128 devices in a mesh: tm: 8 (over y, core), height: 16 (over x, z).
Axes of the slice: x: 4, y: 4, z: 4, core: 2. Of those that a mesh axis runs over, the one named last changes fastest.
Arguments:
- stream: bfloat16 [8, 64, 160, 2240], P('tm', 'height'), may hold values from -6 to 6
- query_tokens: bfloat16 [8, 64, 160, 1120], P('tm', 'height'), may hold values from -6 to 6
- key_tokens: bfloat16 [8, 64, 160, 1120], P('tm', 'height'), may hold values from -6 to 6
- value_tokens: bfloat16 [8, 64, 160, 1120], P('tm', 'height'), may hold values from -12 to 12
- out_weight: bfloat16 [1120, 2240], replicated, may hold values from -0.1875 to 0.1875
- in_weight: bfloat16 [2240, 2, 2800], P(None, None, 'height'), may hold values from -0.125 to 0.125
- conv_weight: float32 [3, 3, 2, 2800], replicated, may hold values from -1.2 to 1.2
Outputs:
- attended: bfloat16 [8, 64, 160, 1120], P('tm', 'height')
- gated: bfloat16 [8, 64, 160, 2800], P('tm', 'height')
The draws below stay inside these ranges and needn't reach their ends.
All inputs are finite; a program needn't handle non-finite values.
Results may differ from the reference program's by a relative error of at most 0.0074.
Values may be sent and summed in bfloat16 or wider, within the bound.
A program may use at most 128 MiB of HBM per device.

```python
import jax
import jax.numpy as jnp
from jax import lax

D = 2240
HD = 112
HEADS = 10
FFH = 2800
WIDTH_TOK = 160
ROWS_DEV = 4
FRAMES = 8
HROWS = 64
HEAD_COLS = 1120


def hot_index(key):
    band_count = HROWS // ROWS_DEV
    window = max(2 * HD // band_count, 2)
    centre = jnp.arange(HROWS, dtype=jnp.int32) // ROWS_DEV * HD // band_count
    jitter = jax.random.randint(jax.random.fold_in(key, 23), (FRAMES, HROWS, WIDTH_TOK, HEADS), 0, window, jnp.int32)
    return (centre[None, :, None, None] + jitter) % HD


def draw_key_tokens(key, part):
    index = hot_index(key)
    base_key, peak_key = jax.random.split(jax.random.fold_in(key, 31))
    shape = (FRAMES, HROWS, WIDTH_TOK, HEADS, HD)
    background = -3.5 + 0.7 * jax.random.normal(base_key, shape, jnp.float32)
    peak = 4.5 + 0.7 * jax.random.normal(peak_key, shape, jnp.float32)
    lanes = jnp.arange(HD, dtype=jnp.int32)
    chosen = lanes == index[..., None]
    result = jnp.clip(jnp.where(chosen, peak, background), -6.0, 6.0)
    return result.reshape(FRAMES, HROWS, WIDTH_TOK, HEADS * HD).astype(jnp.bfloat16)


def draw_query_tokens(key, part):
    first_key, second_key, base_key, peak_key, other_key = jax.random.split(jax.random.fold_in(key, 41), 5)
    index_shape = (FRAMES, HROWS, WIDTH_TOK, HEADS)
    first = jax.random.randint(first_key, index_shape, 0, HD, jnp.int32)
    second = jax.random.randint(second_key, index_shape, 0, HD, jnp.int32)
    shape = (FRAMES, HROWS, WIDTH_TOK, HEADS, HD)
    background = -3.5 + 0.7 * jax.random.normal(base_key, shape, jnp.float32)
    peak = 4.5 + 0.7 * jax.random.normal(peak_key, shape, jnp.float32)
    lesser = 2.5 + 0.7 * jax.random.normal(other_key, shape, jnp.float32)
    lanes = jnp.arange(HD, dtype=jnp.int32)
    result = jnp.where(lanes == second[..., None], lesser, background)
    result = jnp.where(lanes == first[..., None], peak, result)
    result = jnp.clip(result, -6.0, 6.0)
    return result.reshape(FRAMES, HROWS, WIDTH_TOK, HEADS * HD).astype(jnp.bfloat16)


def draw_value_tokens(key, part):
    index = hot_index(key)
    table_key, noise_key, offset_key = jax.random.split(jax.random.fold_in(key, 11), 3)
    shape = (FRAMES, HROWS, WIDTH_TOK, HEADS * HD)
    table = 1.5 * jax.random.normal(table_key, (HEADS, HD, HD), jnp.float32)
    noise = 0.5 * jax.random.normal(noise_key, shape, jnp.float32)
    head_ids = jnp.arange(HEADS, dtype=jnp.int32)[None, None, None, :]
    picked = table[head_ids, index].reshape(shape)
    band_count = HROWS // ROWS_DEV
    offset = jax.random.normal(offset_key, (FRAMES, band_count, 1, 1, HEADS * HD), jnp.float32) * 1.5
    offset = jnp.broadcast_to(offset, (FRAMES, band_count, ROWS_DEV, 1, HEADS * HD)).reshape(FRAMES, HROWS, 1, HEADS * HD)
    return jnp.clip(picked + noise + offset, -12.0, 12.0).astype(jnp.bfloat16)


def level_of(rng, extent, shards, smallest, top_value):
    level, own = 1.0, jax.random.fold_in(rng, 6)
    for axis_at, parts in shards:
        heights = jnp.exp(jax.random.uniform(jax.random.fold_in(own, axis_at), (parts,), jnp.float32, smallest / len(shards), top_value / len(shards)))
        level = level * jnp.repeat(heights, extent[axis_at] // parts).reshape([-1 if axis == axis_at else 1 for axis in range(len(extent))])
    return level


def scatter_about(rng, dims, deviation, bound, shards=(), held_as=jnp.bfloat16):
    entries = jax.random.normal(rng, dims, jnp.float32) * deviation
    if len(shards) > 0:
        entries = level_of(rng, dims, shards, -0.22, 0.18) * entries
    return jnp.clip(entries, min=-bound, max=bound).astype(held_as)


def setup_inputs(seed: int = 0) -> dict:
    key_list = jax.random.split(jax.random.key(seed), 8)
    stream = scatter_about(key_list[0], (FRAMES, HROWS, WIDTH_TOK, D), 1.0, 6.0, ((0, 8), (1, 16)))
    query_tokens = draw_query_tokens(jax.random.fold_in(key_list[7], 71), 0)
    key_tokens = draw_key_tokens(jax.random.fold_in(key_list[7], 71), 0)
    value_tokens = draw_value_tokens(jax.random.fold_in(key_list[7], 71), 0)
    out_weight = scatter_about(key_list[4], (HEAD_COLS, D), HEAD_COLS ** -0.5, 0.1875)
    in_weight = scatter_about(key_list[5], (D, 2, FFH), D ** -0.5, 0.125, ((2, 16),))
    conv_weight = scatter_about(key_list[6], (3, 3, 2, FFH), 0.35, 1.2, (), jnp.float32)
    return dict(stream=stream, query_tokens=query_tokens, key_tokens=key_tokens, value_tokens=value_tokens, out_weight=out_weight, in_weight=in_weight, conv_weight=conv_weight)


def feature(array):
    wide = array.astype(jnp.float32)
    return jnp.where(wide > 0, wide + 1.0, jnp.exp(jnp.minimum(wide, 0.0)))


def depthwise(padded, kernel):
    rows = padded.shape[1] - 2
    columns = padded.shape[2] - 2
    total = jnp.zeros(padded.shape[:1] + (rows, columns) + padded.shape[3:], jnp.float32)
    for row_off in range(3):
        for col_off in range(3):
            total = total + padded[:, row_off:row_off + rows, col_off:col_off + columns].astype(jnp.float32) * kernel[row_off, col_off]
    return (total[..., 0, :] * jax.nn.silu(total[..., 1, :])).astype(jnp.bfloat16)


def reference(stream, query_tokens, key_tokens, value_tokens, out_weight, in_weight, conv_weight):
    frames, hrows, columns, head_cols = query_tokens.shape
    heads = head_cols // HD
    count_tok = hrows * columns
    highest = lax.Precision.HIGHEST
    query_map = feature(query_tokens).reshape(frames, count_tok, heads, HD)
    key_map = feature(key_tokens).reshape(frames, count_tok, heads, HD)
    value_map = value_tokens.astype(jnp.float32).reshape(frames, count_tok, heads, HD)
    states = jnp.einsum("fnha,fnhb->fhab", key_map, value_map, precision=highest)
    norms = jnp.sum(key_map, axis=1)
    states = jnp.cumsum(states, axis=0)
    norms = jnp.cumsum(norms, axis=0)
    numerator = jnp.einsum("fnha,fhab->fnhb", query_map, states, precision=highest)
    denominator = jnp.einsum("fnha,fha->fnh", query_map, norms, precision=highest)
    attended = (numerator / denominator[..., None]).reshape(frames, hrows, columns, head_cols).astype(jnp.bfloat16)
    project = jnp.dot(attended.reshape(-1, head_cols), out_weight, preferred_element_type=jnp.float32)
    mixed = (stream.astype(jnp.float32) + project.reshape(stream.shape)).astype(jnp.bfloat16)
    weight_wide = in_weight.astype(jnp.float32)

    def frame_ffn(mixed_frame):
        expanded = jnp.einsum("rwd,djc->rwjc", mixed_frame.astype(jnp.float32), weight_wide, precision=highest).astype(jnp.bfloat16)
        padded = jnp.pad(expanded, ((1, 1), (1, 1), (0, 0), (0, 0)))
        return depthwise(padded[None], conv_weight)[0]

    gated = lax.map(frame_ffn, mixed)
    return attended, gated
```

```python
import functools

import jax
import jax.numpy as jnp
from jax import lax
from jax.experimental import pallas as pl
from jax.experimental.pallas import tpu as pltpu
from jax.sharding import PartitionSpec as P

HD = 112


def cut_along(x, dim, devices):
    lengths = x.shape
    parts = x.reshape(*lengths[:dim], devices, lengths[dim] // devices, *lengths[dim + 1 :])
    return jnp.moveaxis(parts, dim, 0)


def sent_and_summed(x, axis, dim):
    parts = cut_along(x, dim, lax.axis_size(axis))
    arrived = lax.all_to_all(parts, axis, split_axis=0, concat_axis=0, tiled=True)
    return arrived.sum(axis=0)


def sent_together(arrays, axis, dim, along):
    widths = [a.shape[along] for a in arrays]
    both = jnp.concatenate(arrays, axis=along)
    out = sent_and_summed(both, axis, dim)
    return tuple(jnp.split(out, [sum(widths[:k]) for k in range(1, len(widths))], axis=along))


def collected_together(x, axis):
    leaves = jax.tree.leaves(x)
    turns = sorted(range(len(leaves)), key=lambda k: -leaves[k].size)
    width = (1, *leaves[turns[0]].shape)[-1]
    lines = [
        jnp.pad(leaves[k].reshape(-1), (0, -leaves[k].size % width)).reshape(-1, width)
        for k in turns
    ]
    both, at, found = (lax.all_gather(jnp.concatenate(lines), axis), 0, {})
    for k, line in zip(turns, lines):
        slab = both[:, at : at + len(line)].reshape(len(both), -1)
        found[k] = slab[:, : leaves[k].size].reshape(-1, *leaves[k].shape)
        at += len(line)
    numbers = iter(range(len(leaves)))
    return jax.tree.map(lambda _: found[next(numbers)], x)


def prefix(value, axis, join, neutral):
    count, mine = (lax.axis_size(axis), lax.axis_index(axis))
    pieces = collected_together(value, axis)
    total = jax.tree.map(
        lambda part, zero: jnp.full_like(part, 0) + jnp.asarray(zero, part.dtype), value, neutral
    )

    def turn(position, total):
        longer = join(total, jax.tree.map(lambda part: part[position], pieces))
        return jax.tree.map(lambda new, old: jnp.where(position < mine, new, old), longer, total)

    return lax.fori_loop(0, count - 1, turn, total)


def sent_to_all(x, axis):
    copies = jnp.broadcast_to(x, (lax.axis_size(axis), *x.shape))
    return lax.all_to_all(copies, axis, split_axis=0, concat_axis=0, tiled=True)


def laid_out(parts, dim):
    lengths = list(parts.shape[1:])
    lengths[dim] *= parts.shape[0]
    return jnp.moveaxis(parts, 0, dim).reshape(lengths)


def gathered_copies(x, axis, dim):
    parts = sent_to_all(x, axis)
    return laid_out(parts, dim)


def feature(array):
    wide = array.astype(jnp.float32)
    return jnp.where(wide > 0, wide + 1.0, jnp.exp(jnp.minimum(wide, 0.0)))


def ffn_kernel(m_ref, wa_ref, wb_ref, cw_ref, o_ref, ev, eg):
    nt = (((1,), (1,)), ((), ()))
    for r0 in range(0, 6, 2):
        rows = slice(r0 * 160, (r0 + 2) * 160)
        acc = lax.dot_general(
            m_ref[0, rows], wa_ref[...].reshape(256, 1152), nt, preferred_element_type=jnp.float32
        )
        acc = acc + lax.dot_general(
            m_ref[1, rows], wb_ref[...].reshape(256, 1152), nt, preferred_element_type=jnp.float32
        )
        for r in range(2):
            ev[r0 + r, 8:168] = acc[r * 160 : (r + 1) * 160, :128]
            eg[r0 + r, 8:168] = acc[r * 160 : (r + 1) * 160, 128:]
    zero = jnp.zeros((8, 128), jnp.float32)
    for e in (ev, eg):
        for r in range(6):
            e[r, 0:8] = zero
            e[r, 168:176] = zero
    step = 16
    taps = [
        [jnp.broadcast_to(cw_ref[i * 2 + j : i * 2 + j + 1], (8, 128)) for i in range(9)]
        for j in range(2)
    ]
    for k in range(0, 160, step):
        sums = []
        for e, w in ((ev, taps[0]), (eg, taps[1])):
            acc = [None] * 4
            for r in range(6):
                for b in range(3):
                    x = e[r, k + 7 + b : k + 7 + b + step].reshape(step // 8, 8, 128)
                    for a in range(3):
                        o = r - a
                        if 0 <= o < 4:
                            t = (x * w[a * 3 + b]).reshape(step, 128)
                            acc[o] = t if acc[o] is None else acc[o] + t
            sums.append(acc)
        for o in range(4):
            v, g = sums[0][o], sums[1][o]
            res = (0.5 * v * g) * (1.0 + jnp.tanh(0.5 * g))
            o_ref[o, k : k + step] = res.astype(jnp.bfloat16)


def ffn(m, wa, wb, cw):
    return pl.pallas_call(
        ffn_kernel,
        grid=(22,),
        in_specs=[
            pl.BlockSpec((2, 960, 1152), lambda b: (0, 0, 0)),
            pl.BlockSpec((2, 128, 1152), lambda b: (0, b, 0)),
            pl.BlockSpec((2, 128, 1152), lambda b: (0, b, 0)),
            pl.BlockSpec((18, 128), lambda b: (0, b)),
        ],
        out_specs=pl.BlockSpec((4, 160, 128), lambda b: (0, 0, b)),
        out_shape=jax.ShapeDtypeStruct((4, 160, 2800), jnp.bfloat16),
        scratch_shapes=[pltpu.VMEM((6, 176, 128), jnp.float32)] * 2,
        compiler_params=pltpu.CompilerParams(vmem_limit_bytes=40 * 2**20),
    )(m, wa, wb, cw)


def add_pair(earlier, later):
    return (earlier[0] + later[0], earlier[1] + later[1])


def local(stream, query_tokens, key_tokens, value_tokens, out_weight, in_weight, conv_weight):
    frames_dev, rows_dev, columns, head_cols = query_tokens.shape
    heads = head_cols // HD
    count_tok = rows_dev * columns
    highest = lax.Precision.HIGHEST
    query_map = feature(query_tokens).reshape(frames_dev, count_tok, heads, HD)
    key_map = feature(key_tokens).reshape(frames_dev, count_tok, heads, HD)
    value_map = value_tokens.astype(jnp.float32).reshape(frames_dev, count_tok, heads, HD)
    states = jnp.einsum("fnha,fnhb->fahb", key_map, value_map, precision=highest).reshape(
        frames_dev, HD, head_cols
    )
    norms = jnp.sum(key_map, axis=1).reshape(frames_dev, 1, head_cols)
    states, norms = sent_together((states, norms), "height", 2, 1)
    states = jnp.cumsum(states, axis=0)
    norms = jnp.cumsum(norms, axis=0)
    before = prefix(
        (states[-1], norms[-1]),
        "tm",
        add_pair,
        (jnp.zeros_like(states[-1]), jnp.zeros_like(norms[-1])),
    )
    states = states + before[0]
    norms = norms + before[1]
    states, norms = (gathered_copies(states, "height", 2), gathered_copies(norms, "height", 2))
    numerator = jnp.einsum(
        "fnha,fahb->fnhb", query_map, states.reshape(frames_dev, HD, heads, HD), precision=highest
    )
    denominator = jnp.einsum(
        "fnha,fha->fnh", query_map, norms.reshape(frames_dev, heads, HD), precision=highest
    )
    attended = (
        (numerator / denominator[..., None])
        .reshape(frames_dev, rows_dev, columns, head_cols)
        .astype(jnp.bfloat16)
    )
    project = jnp.dot(
        attended.reshape(-1, head_cols), out_weight, preferred_element_type=jnp.float32
    )
    mixed = (stream.astype(jnp.float32) + project.reshape(stream.shape)).astype(jnp.bfloat16)
    height, tm = lax.axis_index("height"), lax.axis_index("tm")
    core = tm % 2
    heights = lax.axis_size("height")
    wt = jnp.pad(in_weight.transpose(2, 1, 0), ((0, 0), (0, 0), (0, 64)))
    wt = lax.dynamic_slice(wt, (0, 0, core * 1152), (175, 2, 1152))
    after = lax.ppermute(wt[:16], "height", [(i + 1, i) for i in range(heights - 1)])
    wt = lax.dynamic_slice(jnp.concatenate([wt, after]), (height, 0, 0), (176, 2, 1152))
    wa = lax.all_gather(wt.transpose(1, 0, 2), "height", axis=1, tiled=True)
    wb = lax.ppermute(wa, "tm", [(i, i ^ 1) for i in range(8)])
    mixed = mixed[0]
    above = lax.ppermute(mixed[3:], "height", [(i, i + 1) for i in range(heights - 1)])
    below = lax.ppermute(mixed[:1], "height", [(i + 1, i) for i in range(heights - 1)])
    mixed = jnp.concatenate([above, mixed, below]).reshape(960, 2240)
    mixed = jnp.pad(mixed, ((0, 0), (0, 64)))
    mine = lax.dynamic_slice(mixed, (0, core * 1152), (960, 1152))
    other = lax.dynamic_slice(mixed, (0, (1 - core) * 1152), (960, 1152))
    gated = ffn(jnp.stack([mine, other]), wa, wb, conv_weight.reshape(18, 2800))[None]
    return (attended, gated)


def solution(mesh):
    placed = (
        P("tm", "height", None, None),
        P("tm", "height", None, None),
        P("tm", "height", None, None),
        P("tm", "height", None, None),
        P(),
        P(None, None, "height"),
        P(),
    )
    return jax.shard_map(
        local,
        mesh=mesh,
        in_specs=placed,
        out_specs=(P("tm", "height", None, None), P("tm", "height", None, None)),
        check_vma=False,
    )
```

```python
import functools

import jax
import jax.numpy as jnp
from jax import lax
from jax.experimental import pallas as pl
from jax.experimental.pallas import tpu as pltpu
from jax.sharding import PartitionSpec as P

MESH = pl.DeviceIdType.MESH
F32, BF16 = jnp.float32, jnp.bfloat16
HD, TOK, COLS = 112, 640, 1120
SHARD, KH, CH = 176, 1152, 2816
TILES = (
    (0, 256, 0, 384),
    (256, 512, 128, 640),
    (512, 768, 384, 896),
    (768, 1024, 640, 1120),
    (1024, 1120, 896, 1120),
)


def phi(x):
    wide = x.astype(F32)
    return jnp.where(wide > 0, wide + 1.0, jnp.exp(jnp.minimum(wide, 0.0)))


def heads_of(t0, t1):
    return range(t0 // HD, (t1 - 1) // HD + 1)


def lanes_in(head, t0, t1):
    lanes = t0 + lax.broadcasted_iota(jnp.int32, (HD, t1 - t0), 1)
    return (lanes >= head * HD) & (lanes < (head + 1) * HD)


def kernel(
    q_h, k_h, v_h, s_h, ow_h, wp, cw,
    att_out, gated_out, w_all,
    q6, s6, kk, vv, ow, att, mix, own, got, tot, early, full, bd, hd, ev, eg, wbuf, obuf,
    load_sem, halo_s, halo_r, rs_s, rs_r, pre_s, pre_r, ag_s, ag_r,
    ring_s, y_s, dr_s, dy_s, ring_r, y_r, dr_r, dy_r, fill_sem, wb_sem, ob_sem, att_sem,
):
    tm, h = lax.axis_index("tm"), lax.axis_index("height")
    y, c = tm // 2, lax.rem(tm, 2)
    x, z = h // 4, lax.rem(h, 4)
    j0 = lax.rem(y, 2)
    j1 = 1 - j0

    loads = [
        pltpu.make_async_copy(k_h, kk, load_sem.at[0]),
        pltpu.make_async_copy(v_h, vv, load_sem.at[1]),
        pltpu.make_async_copy(q_h, q6.at[160:800], load_sem.at[2]),
        pltpu.make_async_copy(s_h, s6.at[160:800], load_sem.at[3]),
        pltpu.make_async_copy(ow_h, ow, load_sem.at[4]),
    ]
    fill = pltpu.make_async_copy(wp, w_all.at[:, :, pl.ds(pl.multiple_of(h * SHARD, 16), SHARD)], fill_sem)

    barrier = pltpu.get_barrier_semaphore()

    def greet(d, _):
        pl.semaphore_signal(barrier, inc=1, device_id={"tm": tm, "height": lax.rem(h + d, 16)}, device_id_type=MESH)
        return 0

    def greet_tm(d, _):
        pl.semaphore_signal(barrier, inc=1, device_id={"tm": lax.rem(tm + d, 8), "height": h}, device_id_type=MESH)
        return 0

    lax.fori_loop(1, 16, greet, 0)
    lax.fori_loop(1, 8, greet_tm, 0)
    for copy in loads:
        copy.start()
    fill.start()
    pl.semaphore_wait(barrier, 22)

    def send(src, dst, ssem, rsem, to_tm, to_h):
        return pltpu.make_async_remote_copy(
            src_ref=src, dst_ref=dst, send_sem=ssem, recv_sem=rsem,
            device_id={"tm": to_tm, "height": to_h}, device_id_type=MESH,
        )

    def at(dx, zz):
        return lax.rem(x + dx + 4, 4) * 4 + zz

    def zat(dz):
        return lax.rem(z + dz + 4, 4)

    def piece(o, kh, j):
        return w_all.at[kh, j, pl.ds(pl.multiple_of(o * SHARD, 16), SHARD)]

    def ring_send(o, to_h, src=None):
        dst = piece(o, c, j0)
        send(dst if src is None else src, dst, ring_s, ring_r.at[o], tm, to_h).start()

    def ring_wait(o):
        send(piece(o, c, j0), piece(o, c, j0), ring_s, ring_r.at[o], tm, h).wait_recv()

    def pass_on(o):
        low = lax.rem(o, 4) // 2
        yt = lax.rem(y + 3 + 2 * low, 4)
        p = piece(o, c, j0)
        send(p, p, y_s, y_r.at[o], yt * 2 + c, h).start()
        send(p, p, dr_s, dr_r.at[o], y * 2 + 1 - c, h).start()

    def y_take(o):
        p = piece(o, c, j1)
        send(p, p, y_s, y_r.at[o], tm, h).wait_recv()
        send(p, p, dy_s, dy_r.at[o], y * 2 + 1 - c, h).start()

    def d_wait(o):
        p = piece(o, 1 - c, j0)
        send(p, p, dr_s, dr_r.at[o], tm, h).wait_recv()
        p = piece(o, 1 - c, j1)
        send(p, p, dy_s, dy_r.at[o], tm, h).wait_recv()

    def to_x(o, src=None):
        ring_send(o, at(1, z), src)
        ring_send(o, at(-1, z), src)

    mine = wp.at[c, j0]
    dz = 1 - 2 * c
    ring_send(h, x * 4 + zat(1), mine)
    ring_send(h, x * 4 + zat(-1), mine)
    to_x(h, mine)

    own[...] = jnp.zeros(own.shape, F32)
    loads[0].wait()
    for r in range(0, TOK, 160):
        kk[r : r + 160] = phi(kk[r : r + 160]).astype(BF16)
    loads[1].wait()
    norm = jnp.sum(kk[...].astype(F32), axis=0, keepdims=True)
    own[14, :, :COLS] = jnp.broadcast_to(norm, (8, COLS))
    for t0, t1, w0, w1 in TILES:
        part = lax.dot_general(
            kk[:, w0:w1], vv[:, t0:t1], (((0,), (0,)), ((), ())), preferred_element_type=F32
        )
        state = jnp.zeros((HD, t1 - t0), F32)
        for head in heads_of(t0, t1):
            a = head * HD - w0
            state = jnp.where(lanes_in(head, t0, t1), part[a : a + HD], state)
        own[0:14, :, t0:t1] = state.reshape(14, 8, t1 - t0)

    def rs(d, _):
        to = lax.rem(h + d, 16)
        send(own.at[to], got.at[d - 1], rs_s, rs_r, tm, to).start()
        return 0

    lax.fori_loop(1, 16, rs, 0)

    zm, zp, zf = x * 4 + zat(-1), x * 4 + zat(1), x * 4 + zat(2)
    ring_wait(zm)
    ring_wait(zp)
    ring_send(x * 4 + zat(-dz), x * 4 + zat(dz))
    to_x(zm)

    loads[2].wait()
    for r in range(160, 800, 160):
        q6[r : r + 160] = phi(q6[r : r + 160]).astype(BF16)

    send(got, got, rs_s, rs_r, tm, h).wait_recv()
    tot[...] = own[h] + jnp.sum(got[...], axis=0)

    def pre(d, _):
        send(tot, early.at[d - 1], pre_s, pre_r, lax.rem(tm + d, 8), h).start()
        return 0

    lax.fori_loop(1, 8, pre, 0)
    to_x(zp)
    pass_on(zm)
    pass_on(zp)
    send(early, early, pre_s, pre_r, tm, h).wait_recv()
    causal = tot[...]
    for d in range(1, 8):
        causal = causal + jnp.where(d <= tm, early[d - 1], 0.0)
    full[h] = causal

    def ag(d, _):
        to = lax.rem(h + d, 16)
        send(full.at[h], full.at[h], ag_s, ag_r, tm, to).start()
        return 0

    lax.fori_loop(1, 16, ag, 0)

    up, down = lax.rem(h + 15, 16), lax.rem(h + 1, 16)
    halos = [
        send(q_h.at[480:640], q6.at[0:160], halo_s.at[0], halo_r.at[0], tm, down),
        send(q_h.at[0:160], q6.at[800:960], halo_s.at[1], halo_r.at[1], tm, up),
        send(s_h.at[480:640], s6.at[0:160], halo_s.at[2], halo_r.at[2], tm, down),
        send(s_h.at[0:160], s6.at[800:960], halo_s.at[3], halo_r.at[3], tm, up),
    ]
    for copy in halos:
        copy.start()

    ring_wait(zf)
    to_x(zf)
    pass_on(zf)

    def x_event(k):
        zz = zat(k)
        d = 1 - 2 * (zz // 2)
        ring_wait(at(-1, zz))
        ring_wait(at(1, zz))
        ring_send(lax.rem(x - d + 4, 4) * 4 + zz, lax.rem(x + d + 4, 4) * 4 + z)
        pass_on(at(-1, zz))
        pass_on(at(1, zz))

    def far_event(k):
        ring_wait(at(2, zat(k)))
        pass_on(at(2, zat(k)))

    x_event(0)

    send(full.at[0:15], full.at[0:15], ag_s, ag_r, tm, h).wait_recv()
    for i, (t0, t1, w0, w1) in enumerate(TILES):
        bd[i] = jnp.zeros(bd.shape[1:], BF16)
        hd[i] = jnp.zeros(hd.shape[1:], BF16)
        state = full[0:14, :, t0:t1].reshape(HD, t1 - t0)
        for head in heads_of(t0, t1):
            a, inside = head * HD - w0, lanes_in(head, t0, t1)
            bd[i, a : a + HD, : t1 - t0] = jnp.where(inside, state, 0.0).astype(BF16)
            hd[i, a : a + HD, : t1 - t0] = jnp.where(inside, 1.0, 0.0).astype(BF16)
    norms = full[14, 0:1, :COLS]

    def attend(r0, n):
        for i, (t0, t1, w0, w1) in enumerate(TILES):
            qw = q6[r0 : r0 + n, w0:w1]
            b, e = bd[i, : w1 - w0, : t1 - t0], hd[i, : w1 - w0, : t1 - t0]
            qn = qw.astype(F32) * norms[:, w0:w1]
            qa = qn.astype(BF16)
            qb = (qn - qa.astype(F32)).astype(BF16)
            num = jnp.dot(qw, b, preferred_element_type=F32)
            den = jnp.dot(qa, e, preferred_element_type=F32) + jnp.dot(qb, e, preferred_element_type=F32)
            att[r0 : r0 + n, t0:t1] = (num / den).astype(BF16)

    def project(r0, n, keep=None):
        for kh in range(2):
            for a in range(0, KH, 256):
                b = min(a + 256, KH if kh == 0 else 1088)
                cols = slice(kh * KH + a, kh * KH + b)
                p = jnp.dot(att[r0 : r0 + n], ow[:, cols], preferred_element_type=F32)
                p = p + s6[r0 : r0 + n, cols].astype(F32)
                if keep is not None:
                    p = jnp.where(keep, p, 0.0)
                mix[kh, r0 : r0 + n, a:b] = p.astype(BF16)
        mix[1, r0 : r0 + n, 1088:KH] = jnp.zeros((n, KH - 1088), BF16)

    attend(160, 640)
    out_copy = pltpu.make_async_copy(att.at[160:800], att_out, att_sem)
    out_copy.start()
    x_event(-1)
    x_event(1)
    y_take(zm)
    y_take(zp)
    loads[3].wait()
    loads[4].wait()
    project(160, 640)
    y_take(zf)
    x_event(2)
    for copy in halos:
        copy.wait_recv()
    for r, keep in ((0, h > 0), (800, h < 15)):
        q6[r : r + 160] = phi(q6[r : r + 160]).astype(BF16)
        attend(r, 160)
        project(r, 160, keep)

    def block_of(s):
        g = s // 5
        off = jnp.where(g == 2, 3, jnp.where(g == 3, 2, g))
        gx = lax.rem(x + off, 4)
        inner = 11 * (gx // 2) + 6 * lax.rem(gx, 2) + lax.rem(s, 5)
        return jnp.where(s < 20, inner, jnp.where(s == 20, 5, 16))

    def fetch(s):
        b = block_of(s)
        return pltpu.make_async_copy(
            w_all.at[:, :, pl.ds(pl.multiple_of(b * 128, 128), 128)], wbuf.at[lax.rem(s, 2)], wb_sem.at[lax.rem(s, 2)]
        )

    def put(s):
        b = block_of(s)
        return pltpu.make_async_copy(
            obuf.at[lax.rem(s, 2)], gated_out.at[:, :, pl.ds(pl.multiple_of(b * 128, 128), 128)], ob_sem.at[lax.rem(s, 2)]
        )

    zero = jnp.zeros((8, 128), F32)
    for e in (ev, eg):
        for r in range(6):
            e[r, 0:8] = zero
            e[r, 168:176] = zero
    fill.wait()
    d_wait(zm)
    d_wait(zp)
    d_wait(zf)
    fetch(0).start()
    nt = (((1,), (1,)), ((), ()))

    def ready(dx):
        for k in range(4):
            d_wait(at(dx, zat(k)))

    def at_step(s):
        if s == 0:
            y_take(at(-1, z)), y_take(at(1, z)), far_event(0)
        elif s == 1:
            y_take(at(-1, zat(-1))), y_take(at(1, zat(-1)))
        elif s == 2:
            y_take(at(-1, zat(1))), y_take(at(1, zat(1))), far_event(-1)
        elif s == 3:
            y_take(at(-1, zat(2))), y_take(at(1, zat(2))), far_event(1)
        elif s == 4:
            ready(1)
        elif s == 6:
            far_event(2)
        elif s == 8:
            y_take(at(2, z)), y_take(at(2, zat(-1)))
        elif s == 9:
            ready(-1)
        elif s == 12:
            y_take(at(2, zat(1))), y_take(at(2, zat(2)))
        elif s == 14:
            ready(2)

    events = (0, 1, 2, 3, 4, 6, 8, 9, 12, 14)

    def block(s, _):
        for e in events:
            pl.when(s == e)(functools.partial(at_step, e))
        slot = lax.rem(s, 2)

        @pl.when(s < 21)
        def _():
            fetch(s + 1).start()

        fetch(s).wait()
        b = block_of(s)
        for r0 in range(0, 6, 2):
            acc = None
            for kh in range(2):
                w = wbuf[slot, kh].reshape(256, KH)
                t = lax.dot_general(mix[kh, r0 * 160 : (r0 + 2) * 160], w, nt, preferred_element_type=F32)
                acc = t if acc is None else acc + t
            for r in range(2):
                ev[r0 + r, 8:168] = acc[r * 160 : (r + 1) * 160, :128]
                eg[r0 + r, 8:168] = acc[r * 160 : (r + 1) * 160, 128:]

        @pl.when(s >= 2)
        def _():
            put(s - 2).wait()

        lanes = pl.ds(pl.multiple_of(b * 128, 128), 128)
        taps = [
            [jnp.broadcast_to(cw[pl.ds(i * 2 + j, 1), lanes], (8, 128)) for i in range(9)] for j in range(2)
        ]
        step = 16
        for k in range(0, 160, step):
            sums = []
            for e, w in ((ev, taps[0]), (eg, taps[1])):
                acc = [None] * 4
                for r in range(6):
                    for bb in range(3):
                        v = e[r, k + 7 + bb : k + 7 + bb + step].reshape(step // 8, 8, 128)
                        for a in range(3):
                            o = r - a
                            if 0 <= o < 4:
                                t = (v * w[a * 3 + bb]).reshape(step, 128)
                                acc[o] = t if acc[o] is None else acc[o] + t
                sums.append(acc)
            for o in range(4):
                v, g = sums[0][o], sums[1][o]
                res = (0.5 * v * g) * (1.0 + jnp.tanh(0.5 * g))
                obuf[slot, o, k : k + step] = res.astype(BF16)
        put(s).start()
        return 0

    lax.fori_loop(0, 22, block, 0)
    put(20).wait()
    put(21).wait()
    out_copy.wait()
    for copy in halos:
        copy.wait_send()
    send(got, got, rs_s, rs_r, tm, h).wait_send()
    send(early, early, pre_s, pre_r, tm, h).wait_send()
    send(full.at[0:15], full.at[0:15], ag_s, ag_r, tm, h).wait_send()
    whole = w_all.at[0, 0, pl.ds(0, 15 * SHARD)]
    for sem in (ring_s, y_s, dr_s, dy_s):
        send(whole, whole, sem, ring_r.at[0], tm, h).wait_send()


def local(stream, query_tokens, key_tokens, value_tokens, out_weight, in_weight, conv_weight):
    height = lax.axis_index("height")
    heights = lax.axis_size("height")
    wt = in_weight.transpose(2, 1, 0)
    after = lax.ppermute(wt[:16], "height", [(i + 1, i) for i in range(heights - 1)])
    wt = lax.dynamic_slice(jnp.concatenate([wt, after]), (height, 0, 0), (SHARD, 2, 2240))
    wt = jnp.pad(wt, ((0, 0), (0, 0), (0, 64))).transpose(1, 0, 2)
    wp = jnp.stack([wt[:, :, :KH], wt[:, :, KH:]])
    cw = jnp.pad(conv_weight.reshape(18, 2800), ((0, 0), (0, 16)))
    anyspace = pl.BlockSpec(memory_space=pl.ANY)
    vmem = pl.BlockSpec(memory_space=pltpu.VMEM)
    dma, V = pltpu.SemaphoreType.DMA, pltpu.VMEM
    attended, gated, _ = pl.pallas_call(
        kernel,
        in_specs=[anyspace] * 5 + [vmem] * 2,
        out_specs=[anyspace] * 3,
        out_shape=[
            jax.ShapeDtypeStruct((TOK, COLS), BF16),
            jax.ShapeDtypeStruct((4, 160, CH), BF16),
            jax.ShapeDtypeStruct((2, 2, CH, KH), BF16),
        ],
        scratch_shapes=[
            V((960, COLS), BF16), V((960, 2240), BF16), V((TOK, COLS), BF16), V((TOK, COLS), BF16),
            V((COLS, 2240), BF16), V((960, COLS), BF16), V((2, 960, KH), BF16),
            V((16, 8, KH), F32), V((15, 8, KH), F32), V((8, KH), F32), V((7, 8, KH), F32), V((16, 8, KH), F32),
            V((5, 512, 256), BF16), V((5, 512, 256), BF16),
            V((6, 176, 128), F32), V((6, 176, 128), F32),
            V((2, 2, 2, 128, KH), BF16), V((2, 4, 160, 128), BF16),
            dma((5,)), dma((4,)), dma((4,)),
            dma, dma, dma, dma, dma, dma,
            dma, dma, dma, dma, dma((16,)), dma((16,)), dma((16,)), dma((16,)),
            dma, dma((2,)), dma((2,)), dma,
        ],
        compiler_params=pltpu.CompilerParams(
            collective_id=0, has_side_effects=True, vmem_limit_bytes=60 * 2**20
        ),
    )(
        query_tokens.reshape(TOK, COLS), key_tokens.reshape(TOK, COLS), value_tokens.reshape(TOK, COLS),
        stream.reshape(TOK, 2240), out_weight, wp, cw,
    )
    return attended.reshape(1, 4, 160, COLS), gated[None, :, :, :2800]


def solution(mesh):
    rows = P("tm", "height", None, None)
    return jax.shard_map(
        local,
        mesh=mesh,
        in_specs=(rows, rows, rows, rows, P(), P(None, None, "height"), P()),
        out_specs=(rows, rows),
        check_vma=False,
    )
```

```python
import functools

import jax
import jax.numpy as jnp
from jax import lax
from jax.experimental import pallas as pl
from jax.experimental.pallas import tpu as pltpu
from jax.sharding import PartitionSpec as P

MESH = pl.DeviceIdType.MESH
F32, BF16 = jnp.float32, jnp.bfloat16
HD, TOK, COLS = 112, 640, 1120
SHARD, KH, CH = 176, 1152, 2816
TILES = (
    (0, 256, 0, 384),
    (256, 512, 128, 640),
    (512, 768, 384, 896),
    (768, 1024, 640, 1120),
    (1024, 1120, 896, 1120),
)


def phi(x):
    wide = x.astype(F32)
    return jnp.where(wide > 0, wide + 1.0, jnp.exp(jnp.minimum(wide, 0.0)))


def heads_of(t0, t1):
    return range(t0 // HD, (t1 - 1) // HD + 1)


def lanes_in(head, t0, t1):
    lanes = t0 + lax.broadcasted_iota(jnp.int32, (HD, t1 - t0), 1)
    return (lanes >= head * HD) & (lanes < (head + 1) * HD)


def kernel(
    q_h, k_h, v_h, s_h, ow_h, wa_h, wb_h, cw,
    att_out, gated_out, w_all,
    q6, s6, kk, vv, ow, wp, wx, att, mix, own, got, tot, early, full, bd, hd, ev, eg, wbuf, obuf,
    load_sem, halo_s, halo_r, rs_s, rs_r, pre_s, pre_r, ag_s, ag_r,
    ring_s, y_s, dr_s, dy_s, ring_r, y_r, dr_r, dy_r, fill_sem, wb_sem, ob_sem, att_sem, edge_s, edge_r,
):
    tm, h = lax.axis_index("tm"), lax.axis_index("height")
    y, c = tm // 2, lax.rem(tm, 2)
    x, z = h // 4, lax.rem(h, 4)
    j0 = lax.rem(y, 2)
    j1 = 1 - j0

    loads = [
        pltpu.make_async_copy(k_h, kk, load_sem.at[0]),
        pltpu.make_async_copy(v_h, vv, load_sem.at[1]),
        pltpu.make_async_copy(q_h, q6.at[0:640], load_sem.at[2]),
        pltpu.make_async_copy(s_h, s6.at[0:640], load_sem.at[3]),
        pltpu.make_async_copy(ow_h, ow, load_sem.at[4]),
        pltpu.make_async_copy(wa_h, wp, load_sem.at[5]),
    ]
    fill = pltpu.make_async_copy(wp, w_all.at[:, :, pl.ds(pl.multiple_of(h * SHARD, 16), SHARD)], fill_sem)

    barrier = pltpu.get_barrier_semaphore()

    def greet(d, _):
        pl.semaphore_signal(barrier, inc=1, device_id={"tm": tm, "height": lax.rem(h + d, 16)}, device_id_type=MESH)
        return 0

    def greet_tm(d, _):
        pl.semaphore_signal(barrier, inc=1, device_id={"tm": lax.rem(tm + d, 8), "height": h}, device_id_type=MESH)
        return 0

    lax.fori_loop(1, 16, greet, 0)
    lax.fori_loop(1, 8, greet_tm, 0)
    for i in (5, 0, 1, 2, 3, 4):
        loads[i].start()
    pl.semaphore_wait(barrier, 22)
    up, down = lax.rem(h + 15, 16), lax.rem(h + 1, 16)

    def send(src, dst, ssem, rsem, to_tm, to_h):
        return pltpu.make_async_remote_copy(
            src_ref=src, dst_ref=dst, send_sem=ssem, recv_sem=rsem,
            device_id={"tm": to_tm, "height": to_h}, device_id_type=MESH,
        )

    def at(dx, zz):
        return lax.rem(x + dx + 4, 4) * 4 + zz

    def zat(dz):
        return lax.rem(z + dz + 4, 4)

    def piece(o, kh, j):
        return w_all.at[kh, j, pl.ds(pl.multiple_of(o * SHARD, 16), SHARD)]

    def ring_send(o, to_h, src=None):
        dst = piece(o, c, j0)
        send(dst if src is None else src, dst, ring_s, ring_r.at[o], tm, to_h).start()

    def ring_wait(o):
        send(piece(o, c, j0), piece(o, c, j0), ring_s, ring_r.at[o], tm, h).wait_recv()

    def pass_on(o, over_y=True):
        low = lax.rem(o // 8 + lax.rem(o, 4) // 2, 2)
        yt = lax.rem(y + 3 + 2 * low, 4)
        p = piece(o, c, j0)
        if over_y:
            send(p, p, y_s, y_r.at[o], yt * 2 + c, h).start()
        send(p, p, dr_s, dr_r.at[o], y * 2 + 1 - c, h).start()

    def y_take(o):
        p = piece(o, c, j1)
        send(p, p, y_s, y_r.at[o], tm, h).wait_recv()
        send(p, p, dy_s, dy_r.at[o], y * 2 + 1 - c, h).start()

    def d_wait(o):
        p = piece(o, 1 - c, j0)
        send(p, p, dr_s, dr_r.at[o], tm, h).wait_recv()
        p = piece(o, 1 - c, j1)
        send(p, p, dy_s, dy_r.at[o], tm, h).wait_recv()

    def to_x(o, src=None):
        ring_send(o, at(1, z), src)
        ring_send(o, at(-1, z), src)

    edge = send(wb_h, wx, edge_s, edge_r, tm, up)
    edge.start()
    own[...] = jnp.zeros(own.shape, BF16)
    loads[5].wait()
    edge.wait_recv()
    wp[:, :, 160:176] = wp[:, :, 160:176] + wx[...]
    loads[0].wait()
    for r in range(0, TOK, 160):
        kk[r : r + 160] = phi(kk[r : r + 160]).astype(BF16)
    mine = wp.at[c, j0]
    dz = 1 - 2 * c
    ring_send(h, x * 4 + zat(1), mine)
    ring_send(h, x * 4 + zat(-1), mine)
    to_x(h, mine)
    fill.start()

    loads[1].wait()
    norm = jnp.sum(kk[...].astype(F32), axis=0, keepdims=True)
    own[14, :, :COLS] = jnp.broadcast_to(norm, (8, COLS)).astype(BF16)
    for t0, t1, w0, w1 in TILES:
        part = lax.dot_general(
            kk[:, w0:w1], vv[:, t0:t1], (((0,), (0,)), ((), ())), preferred_element_type=F32
        )
        state = jnp.zeros((HD, t1 - t0), F32)
        for head in heads_of(t0, t1):
            a = head * HD - w0
            state = jnp.where(lanes_in(head, t0, t1), part[a : a + HD], state)
        own[0:14, :, t0:t1] = state.reshape(14, 8, t1 - t0).astype(BF16)

    def rs(d, _):
        to = lax.rem(h + d, 16)
        send(own.at[to], got.at[d - 1], rs_s, rs_r, tm, to).start()
        return 0

    lax.fori_loop(1, 16, rs, 0)

    zm, zp, zf = x * 4 + zat(-1), x * 4 + zat(1), x * 4 + zat(2)
    loads[2].wait()
    for r in range(0, TOK, 160):
        q6[r : r + 160] = phi(q6[r : r + 160]).astype(BF16)
    ring_wait(zm)
    ring_wait(zp)
    ring_send(x * 4 + zat(-dz), x * 4 + zat(dz))

    send(got, got, rs_s, rs_r, tm, h).wait_recv()
    tot[...] = own[h].astype(F32) + jnp.sum(got[...].astype(F32), axis=0)

    def pre(d, _):
        send(tot, early.at[d - 1], pre_s, pre_r, lax.rem(tm + d, 8), h).start()
        return 0

    lax.fori_loop(1, 8, pre, 0)
    halos = [
        send(q_h.at[480:640], q6.at[640:800], halo_s.at[0], halo_r.at[0], tm, down),
        send(q_h.at[0:160], q6.at[800:960], halo_s.at[1], halo_r.at[1], tm, up),
        send(s_h.at[480:640], s6.at[640:800], halo_s.at[2], halo_r.at[2], tm, down),
        send(s_h.at[0:160], s6.at[800:960], halo_s.at[3], halo_r.at[3], tm, up),
    ]
    halos[0].start()
    halos[1].start()
    pass_on(zm)
    pass_on(zp)
    send(early, early, pre_s, pre_r, tm, h).wait_recv()
    causal = tot[...]
    for d in range(1, 8):
        causal = causal + jnp.where(d <= tm, early[d - 1], 0.0)
    high = causal.astype(BF16)
    rest = (causal - high.astype(F32)).astype(BF16)
    odd = lax.broadcasted_iota(jnp.int32, causal.shape, 0) == 1
    full[h] = jnp.where(odd & (h == 14), rest.astype(F32), high.astype(F32)).astype(BF16)

    def ag(d, _):
        to = lax.rem(h + d, 16)
        send(full.at[h], full.at[h], ag_s, ag_r, tm, to).start()
        return 0

    lax.fori_loop(1, 16, ag, 0)
    halos[2].start()
    halos[3].start()

    def x_event(k):
        zz = zat(k)
        d = 1 - 2 * (zz // 2)
        ring_wait(at(-1, zz))
        ring_wait(at(1, zz))
        ring_send(lax.rem(x - d + 4, 4) * 4 + zz, lax.rem(x + d + 4, 4) * 4 + z)
        pass_on(at(-1, zz), k != 0)
        pass_on(at(1, zz), k != 0)

    def far_event(k):
        ring_wait(at(2, zat(k)))
        pass_on(at(2, zat(k)))

    x_event(0)
    to_x(zm)
    to_x(zp)
    ring_wait(zf)
    to_x(zf)
    pass_on(zf)
    for to in (at(1, z), at(-1, z)):
        send(wp.at[c, j1], piece(h, c, j1), y_s, y_r.at[h], tm, to).start()

    send(full.at[0:15], full.at[0:15], ag_s, ag_r, tm, h).wait_recv()
    for i, (t0, t1, w0, w1) in enumerate(TILES):
        bd[i] = jnp.zeros(bd.shape[1:], BF16)
        hd[i] = jnp.zeros(hd.shape[1:], BF16)
        state = full[0:14, :, t0:t1].astype(F32).reshape(HD, t1 - t0)
        for head in heads_of(t0, t1):
            a, inside = head * HD - w0, lanes_in(head, t0, t1)
            bd[i, a : a + HD, : t1 - t0] = jnp.where(inside, state, 0.0).astype(BF16)
            hd[i, a : a + HD, : t1 - t0] = jnp.where(inside, 1.0, 0.0).astype(BF16)
    norms = full[14, 0:1, :COLS].astype(F32) + full[14, 1:2, :COLS].astype(F32)

    def attend(r0, n):
        for i, (t0, t1, w0, w1) in enumerate(TILES):
            qw = q6[r0 : r0 + n, w0:w1]
            b, e = bd[i, : w1 - w0, : t1 - t0], hd[i, : w1 - w0, : t1 - t0]
            qn = qw.astype(F32) * norms[:, w0:w1]
            qa = qn.astype(BF16)
            qb = (qn - qa.astype(F32)).astype(BF16)
            num = jnp.dot(qw, b, preferred_element_type=F32)
            den = jnp.dot(qa, e, preferred_element_type=F32) + jnp.dot(qb, e, preferred_element_type=F32)
            att[r0 : r0 + n, t0:t1] = (num / den).astype(BF16)

    def project(r0, n, edges=False):
        for kh in range(2):
            for a in range(0, KH, 256):
                b = min(a + 256, KH if kh == 0 else 1088)
                cols = slice(kh * KH + a, kh * KH + b)
                p = jnp.dot(att[r0 : r0 + n], ow[:, cols], preferred_element_type=F32)
                p = p + s6[r0 : r0 + n, cols].astype(F32)
                if edges:
                    p = jnp.concatenate([jnp.where(h > 0, p[:160], 0.0), jnp.where(h < 15, p[160:], 0.0)])
                mix[kh, r0 : r0 + n, a:b] = p.astype(BF16)
        mix[1, r0 : r0 + n, 1088:KH] = jnp.zeros((n, KH - 1088), BF16)

    attend(0, 640)
    out_copy = pltpu.make_async_copy(att.at[0:640], att_out, att_sem)
    out_copy.start()
    y_take(zm)
    y_take(zp)
    far_event(0)
    loads[3].wait()
    loads[4].wait()
    project(0, 640)
    x_event(-1)
    y_take(zf)
    halos[0].wait_recv()
    halos[1].wait_recv()
    for r in (640, 800):
        q6[r : r + 160] = phi(q6[r : r + 160]).astype(BF16)
    attend(640, 320)
    halos[2].wait_recv()
    halos[3].wait_recv()
    project(640, 320, True)
    x_event(1)

    def block_of(s):
        g = s // 5
        off = jnp.where(g == 2, 3, jnp.where(g == 3, 2, g))
        gx = lax.rem(x + off, 4)
        inner = 11 * (gx // 2) + 6 * lax.rem(gx, 2) + lax.rem(s, 5)
        return jnp.where(s < 20, inner, jnp.where(s == 20, 5, 16))

    def fetch(s):
        b = block_of(s)
        return pltpu.make_async_copy(
            w_all.at[:, :, pl.ds(pl.multiple_of(b * 128, 128), 128)], wbuf.at[lax.rem(s, 2)], wb_sem.at[lax.rem(s, 2)]
        )

    def put(s):
        b = block_of(s)
        return pltpu.make_async_copy(
            obuf.at[lax.rem(s, 2)], gated_out.at[:, :, pl.ds(pl.multiple_of(b * 128, 128), 128)], ob_sem.at[lax.rem(s, 2)]
        )

    zero = jnp.zeros((8, 128), F32)
    for e in (ev, eg):
        for r in range(6):
            e[r, 0:8] = zero
            e[r, 168:176] = zero
    fill.wait()
    d_wait(zm)
    d_wait(zp)
    d_wait(zf)
    fetch(0).start()
    nt = (((1,), (1,)), ((), ()))

    def ready(dx):
        for k in range(4):
            d_wait(at(dx, zat(k)))

    def at_step(s):
        if s == 0:
            y_take(at(-1, z)), y_take(at(1, z))
        elif s == 1:
            far_event(-1)
        elif s == 2:
            y_take(at(-1, zat(-1))), y_take(at(1, zat(-1)))
        elif s == 3:
            x_event(2)
        elif s == 4:
            y_take(at(-1, zat(1))), y_take(at(1, zat(1))), far_event(1)
            y_take(at(-1, zat(2))), y_take(at(1, zat(2))), ready(1)
        elif s == 6:
            far_event(2)
        elif s == 7:
            y_take(at(2, z)), y_take(at(2, zat(-1)))
        elif s == 9:
            ready(-1)
        elif s == 11:
            y_take(at(2, zat(1)))
        elif s == 12:
            y_take(at(2, zat(2)))
        elif s == 14:
            ready(2)

    events = (0, 1, 2, 3, 4, 6, 7, 9, 11, 12, 14)

    def block(s, _):
        for e in events:
            pl.when(s == e)(functools.partial(at_step, e))
        slot = lax.rem(s, 2)

        @pl.when(s < 21)
        def _():
            fetch(s + 1).start()

        fetch(s).wait()
        b = block_of(s)
        for r0, pair in ((0, (1, 2)), (2, (3, 4)), (4, (0, 5))):
            acc = None
            for kh in range(2):
                w = wbuf[slot, kh].reshape(256, KH)
                t = lax.dot_general(mix[kh, r0 * 160 : (r0 + 2) * 160], w, nt, preferred_element_type=F32)
                acc = t if acc is None else acc + t
            for i, r in enumerate(pair):
                ev[r, 8:168] = acc[i * 160 : (i + 1) * 160, :128]
                eg[r, 8:168] = acc[i * 160 : (i + 1) * 160, 128:]

        @pl.when(s >= 2)
        def _():
            put(s - 2).wait()

        lanes = pl.ds(pl.multiple_of(b * 128, 128), 128)
        taps = [
            [jnp.broadcast_to(cw[pl.ds(i * 2 + j, 1), lanes], (8, 128)) for i in range(9)] for j in range(2)
        ]
        step = 16
        for k in range(0, 160, step):
            sums = []
            for e, w in ((ev, taps[0]), (eg, taps[1])):
                acc = [None] * 4
                for r in range(6):
                    for bb in range(3):
                        v = e[r, k + 7 + bb : k + 7 + bb + step].reshape(step // 8, 8, 128)
                        for a in range(3):
                            o = r - a
                            if 0 <= o < 4:
                                t = (v * w[a * 3 + bb]).reshape(step, 128)
                                acc[o] = t if acc[o] is None else acc[o] + t
                sums.append(acc)
            for o in range(4):
                v, g = sums[0][o], sums[1][o]
                res = (0.5 * v * g) * (1.0 + jnp.tanh(0.5 * g))
                obuf[slot, o, k : k + step] = res.astype(BF16)
        put(s).start()
        return 0

    lax.fori_loop(0, 22, block, 0)
    put(20).wait()
    put(21).wait()
    out_copy.wait()
    edge.wait_send()
    for copy in halos:
        copy.wait_send()
    send(got, got, rs_s, rs_r, tm, h).wait_send()
    send(early, early, pre_s, pre_r, tm, h).wait_send()
    send(full.at[0:15], full.at[0:15], ag_s, ag_r, tm, h).wait_send()
    whole = w_all.at[0, 0, pl.ds(0, 15 * SHARD)]
    for sem in (ring_s, y_s, dr_s, dy_s):
        send(whole, whole, sem, ring_r.at[0], tm, h).wait_send()


def local(stream, query_tokens, key_tokens, value_tokens, out_weight, in_weight, conv_weight):
    height = lax.axis_index("height")
    wt = jnp.pad(in_weight.transpose(2, 1, 0), ((16, 16), (0, 0), (0, 64)))
    wt = wt.reshape(207, 2, 2, KH)
    wa = lax.dynamic_slice(wt, (16 + height, 0, 0, 0), (SHARD, 2, 2, KH)).transpose(2, 1, 0, 3)
    wb = lax.dynamic_slice(wt, (height, 0, 0, 0), (16, 2, 2, KH)).transpose(2, 1, 0, 3)
    cw = jnp.pad(conv_weight.reshape(18, 2800), ((0, 0), (0, 16)))
    anyspace = pl.BlockSpec(memory_space=pl.ANY)
    vmem = pl.BlockSpec(memory_space=pltpu.VMEM)
    dma, V = pltpu.SemaphoreType.DMA, pltpu.VMEM
    attended, gated, _ = pl.pallas_call(
        kernel,
        in_specs=[anyspace] * 7 + [vmem],
        out_specs=[anyspace] * 3,
        out_shape=[
            jax.ShapeDtypeStruct((TOK, COLS), BF16),
            jax.ShapeDtypeStruct((4, 160, CH), BF16),
            jax.ShapeDtypeStruct((2, 2, CH, KH), BF16),
        ],
        scratch_shapes=[
            V((960, COLS), BF16), V((960, 2240), BF16), V((TOK, COLS), BF16), V((TOK, COLS), BF16),
            V((COLS, 2240), BF16), V((2, 2, SHARD, KH), BF16), V((2, 2, 16, KH), BF16), V((960, COLS), BF16), V((2, 960, KH), BF16),
            V((16, 8, KH), BF16), V((15, 8, KH), BF16), V((8, KH), F32), V((7, 8, KH), F32), V((16, 8, KH), BF16),
            V((5, 512, 256), BF16), V((5, 512, 256), BF16),
            V((6, 176, 128), F32), V((6, 176, 128), F32),
            V((2, 2, 2, 128, KH), BF16), V((2, 4, 160, 128), BF16),
            dma((6,)), dma((4,)), dma((4,)),
            dma, dma, dma, dma, dma, dma,
            dma, dma, dma, dma, dma((16,)), dma((16,)), dma((16,)), dma((16,)),
            dma, dma((2,)), dma((2,)), dma, dma, dma,
        ],
        compiler_params=pltpu.CompilerParams(
            collective_id=0, has_side_effects=True, vmem_limit_bytes=60 * 2**20
        ),
    )(
        query_tokens.reshape(TOK, COLS), key_tokens.reshape(TOK, COLS), value_tokens.reshape(TOK, COLS),
        stream.reshape(TOK, 2240), out_weight, wa, wb, cw,
    )
    return attended.reshape(1, 4, 160, COLS), gated[None, :, :, :2800]


def solution(mesh):
    rows = P("tm", "height", None, None)
    return jax.shard_map(
        local,
        mesh=mesh,
        in_specs=(rows, rows, rows, rows, P(), P(None, None, "height"), P()),
        out_specs=(rows, rows),
        check_vma=False,
    )
```

```python
import functools

import jax
import jax.numpy as jnp
from jax import lax
from jax.experimental import pallas as pl
from jax.experimental.pallas import tpu as pltpu
from jax.sharding import PartitionSpec as P

MESH = pl.DeviceIdType.MESH
F32, BF16 = jnp.float32, jnp.bfloat16
HD, TOK, COLS = 112, 640, 1120
SHARD, KH, CH = 176, 1152, 2816
TILES = (
    (0, 256, 0, 384),
    (256, 512, 128, 640),
    (512, 768, 384, 896),
    (768, 1024, 640, 1120),
    (1024, 1120, 896, 1120),
)


def phi(x):
    wide = x.astype(F32)
    return jnp.where(wide > 0, wide + 1.0, jnp.exp(jnp.minimum(wide, 0.0)))


def heads_of(t0, t1):
    return range(t0 // HD, (t1 - 1) // HD + 1)


def lanes_in(head, t0, t1):
    lanes = t0 + lax.broadcasted_iota(jnp.int32, (HD, t1 - t0), 1)
    return (lanes >= head * HD) & (lanes < (head + 1) * HD)


def kernel(
    q_h, k_h, v_h, s_h, ow_h, wa_h, wb_h, cw,
    att_out, gated_out, w_all,
    q6, s6, kk, kt, vv, ow, wp, wx, att, mix, own, got, tot, early, full, bd, hd, ev, eg, wbuf, obuf,
    load_sem, halo_s, halo_r, rs_s, rs_r, pre_s, pre_r, ag_s, ag_r,
    ring_s, y_s, dr_s, dy_s, ring_r, y_r, dr_r, dy_r, fill_sem, wb_sem, ob_sem, att_sem, edge_s, edge_r,
):
    tm, h = lax.axis_index("tm"), lax.axis_index("height")
    y, c = tm // 2, lax.rem(tm, 2)
    x, z = h // 4, lax.rem(h, 4)
    j0 = lax.rem(y, 2)
    j1 = 1 - j0

    loads = [
        pltpu.make_async_copy(k_h, kk, load_sem.at[0]),
        pltpu.make_async_copy(v_h, vv, load_sem.at[1]),
        pltpu.make_async_copy(q_h, q6.at[0:640], load_sem.at[2]),
        pltpu.make_async_copy(s_h, s6.at[0:640], load_sem.at[3]),
        pltpu.make_async_copy(ow_h, ow, load_sem.at[4]),
        pltpu.make_async_copy(wa_h, wp, load_sem.at[5]),
    ]
    fill = pltpu.make_async_copy(wp, w_all.at[:, :, pl.ds(pl.multiple_of(h * SHARD, 16), SHARD)], fill_sem)

    barrier = pltpu.get_barrier_semaphore()

    def greet(d, _):
        pl.semaphore_signal(barrier, inc=1, device_id={"tm": tm, "height": lax.rem(h + d, 16)}, device_id_type=MESH)
        return 0

    def greet_tm(d, _):
        pl.semaphore_signal(barrier, inc=1, device_id={"tm": lax.rem(tm + d, 8), "height": h}, device_id_type=MESH)
        return 0

    lax.fori_loop(1, 16, greet, 0)
    lax.fori_loop(1, 8, greet_tm, 0)
    for i in (5, 0, 1, 2, 3, 4):
        loads[i].start()
    pl.semaphore_wait(barrier, 22)
    up, down = lax.rem(h + 15, 16), lax.rem(h + 1, 16)

    def send(src, dst, ssem, rsem, to_tm, to_h):
        return pltpu.make_async_remote_copy(
            src_ref=src, dst_ref=dst, send_sem=ssem, recv_sem=rsem,
            device_id={"tm": to_tm, "height": to_h}, device_id_type=MESH,
        )

    def at(dx, zz):
        return lax.rem(x + dx + 4, 4) * 4 + zz

    def zat(dz):
        return lax.rem(z + dz + 4, 4)

    def piece(o, kh, j):
        return w_all.at[kh, j, pl.ds(pl.multiple_of(o * SHARD, 16), SHARD)]

    def ring_send(o, to_h, src=None):
        dst = piece(o, c, j0)
        send(dst if src is None else src, dst, ring_s, ring_r.at[o], tm, to_h).start()

    def ring_wait(o):
        send(piece(o, c, j0), piece(o, c, j0), ring_s, ring_r.at[o], tm, h).wait_recv()

    def pass_on(o, over_y=True):
        low = lax.rem(o // 8 + lax.rem(o, 4) // 2, 2)
        yt = lax.rem(y + 3 + 2 * low, 4)
        p = piece(o, c, j0)
        if over_y:
            send(p, p, y_s, y_r.at[o], yt * 2 + c, h).start()
        send(p, p, dr_s, dr_r.at[o], y * 2 + 1 - c, h).start()

    def y_take(o):
        p = piece(o, c, j1)
        send(p, p, y_s, y_r.at[o], tm, h).wait_recv()
        send(p, p, dy_s, dy_r.at[o], y * 2 + 1 - c, h).start()

    def d_wait(o):
        p = piece(o, 1 - c, j0)
        send(p, p, dr_s, dr_r.at[o], tm, h).wait_recv()
        p = piece(o, 1 - c, j1)
        send(p, p, dy_s, dy_r.at[o], tm, h).wait_recv()

    def to_x(o, src=None):
        ring_send(o, at(1, z), src)
        ring_send(o, at(-1, z), src)

    def x_take(k):
        zz = zat(k)
        ring_wait(at(-1, zz))
        ring_wait(at(1, zz))
        pass_on(at(-1, zz))
        pass_on(at(1, zz))

    def x_turn(k):
        zz = zat(k)
        limit = jnp.where(z == 0, 3, jnp.where(z == 3, 1, 2))
        d = jnp.where(zz < limit, 1, -1)
        ring_send(lax.rem(x - d + 4, 4) * 4 + zz, lax.rem(x + d + 4, 4) * 4 + z)

    def x_event(k):
        x_take(k)
        x_turn(k)

    edge = send(wb_h, wx, edge_s, edge_r, tm, up)
    edge.start()
    own[...] = jnp.zeros(own.shape, BF16)
    loads[5].wait()
    edge.wait_recv()
    wp[:, :, 160:176] = wp[:, :, 160:176] + wx[...]
    loads[0].wait()
    for r in range(0, TOK, 160):
        kk[r : r + 160] = phi(kk[r : r + 160]).astype(BF16)
    mine = wp.at[c, j0]
    dz = 1 - 2 * c
    ring_send(h, x * 4 + zat(1), mine)
    ring_send(h, x * 4 + zat(-1), mine)
    to_x(h, mine)
    for d in (1, -1):
        send(wp.at[c, j1], piece(h, c, j1), y_s, y_r.at[h], tm, x * 4 + zat(d)).start()
    fill.start()

    loads[1].wait()
    norm = jnp.sum(kk[...].astype(F32), axis=0, keepdims=True)
    own[14, :, :COLS] = jnp.broadcast_to(norm, (8, COLS)).astype(BF16)
    for a in range(0, COLS, 128):
        b = min(a + 128, COLS)
        kt[a:b] = kk[:, a:b].T
    zm, zp, zf = x * 4 + zat(-1), x * 4 + zat(1), x * 4 + zat(2)
    for i, (t0, t1, w0, w1) in enumerate(TILES):
        part = jnp.dot(kt[w0:w1], vv[:, t0:t1], preferred_element_type=F32)
        state = jnp.zeros((HD, t1 - t0), F32)
        for head in heads_of(t0, t1):
            a = head * HD - w0
            state = jnp.where(lanes_in(head, t0, t1), part[a : a + HD], state)
        own[0:14, :, t0:t1] = state.reshape(14, 8, t1 - t0).astype(BF16)

    def rs(d, _):
        to = lax.rem(h + d, 16)
        send(own.at[to], got.at[d - 1], rs_s, rs_r, tm, to).start()
        return 0

    lax.fori_loop(1, 16, rs, 0)
    ring_wait(zm)
    ring_wait(zp)
    ring_send(x * 4 + zat(-dz), x * 4 + zat(dz))
    to_x(zm)
    pass_on(zm, False)
    x_take(0)

    to_x(zp)
    pass_on(zp, False)
    y_take(zm)
    y_take(zp)
    turn = piece(x * 4 + zat(-dz), c, j1)
    send(turn, turn, y_s, y_r.at[x * 4 + zat(-dz)], tm, x * 4 + zat(dz)).start()
    loads[2].wait()
    for r in range(0, TOK, 160):
        q6[r : r + 160] = phi(q6[r : r + 160]).astype(BF16)

    send(got, got, rs_s, rs_r, tm, h).wait_recv()
    tot[...] = own[h].astype(F32) + jnp.sum(got[...].astype(F32), axis=0)

    def pre(d, _):
        send(tot, early.at[d - 1], pre_s, pre_r, lax.rem(tm + d, 8), h).start()
        return 0

    lax.fori_loop(1, 8, pre, 0)
    halos = [
        send(q_h.at[480:640], q6.at[640:800], halo_s.at[0], halo_r.at[0], tm, down),
        send(q_h.at[0:160], q6.at[800:960], halo_s.at[1], halo_r.at[1], tm, up),
        send(s_h.at[480:640], s6.at[640:800], halo_s.at[2], halo_r.at[2], tm, down),
        send(s_h.at[0:160], s6.at[800:960], halo_s.at[3], halo_r.at[3], tm, up),
    ]
    halos[0].start()
    halos[1].start()
    x_take(-1)
    send(early, early, pre_s, pre_r, tm, h).wait_recv()
    causal = tot[...]
    for d in range(1, 8):
        causal = causal + jnp.where(d <= tm, early[d - 1], 0.0)
    high = causal.astype(BF16)
    rest = (causal - high.astype(F32)).astype(BF16)
    odd = lax.broadcasted_iota(jnp.int32, causal.shape, 0) == 1
    full[h] = jnp.where(odd & (h == 14), rest.astype(F32), high.astype(F32)).astype(BF16)

    def ag(d, _):
        to = lax.rem(h + d, 16)
        send(full.at[h], full.at[h], ag_s, ag_r, tm, to).start()
        return 0

    lax.fori_loop(1, 16, ag, 0)
    halos[2].start()
    halos[3].start()

    def far_event(k):
        ring_wait(at(2, zat(k)))
        pass_on(at(2, zat(k)))

    x_turn(0)
    x_turn(-1)
    ring_wait(zf)
    to_x(zf)
    pass_on(zf, False)
    x_event(1)

    send(full.at[0:15], full.at[0:15], ag_s, ag_r, tm, h).wait_recv()
    for i, (t0, t1, w0, w1) in enumerate(TILES):
        bd[i] = jnp.zeros(bd.shape[1:], BF16)
        hd[i] = jnp.zeros(hd.shape[1:], BF16)
        state = full[0:14, :, t0:t1].astype(F32).reshape(HD, t1 - t0)
        for head in heads_of(t0, t1):
            a, inside = head * HD - w0, lanes_in(head, t0, t1)
            bd[i, a : a + HD, : t1 - t0] = jnp.where(inside, state, 0.0).astype(BF16)
            hd[i, a : a + HD, : t1 - t0] = jnp.where(inside, 1.0, 0.0).astype(BF16)
    norms = full[14, 0:1, :COLS].astype(F32) + full[14, 1:2, :COLS].astype(F32)

    def attend(r0, n):
        for i, (t0, t1, w0, w1) in enumerate(TILES):
            qw = q6[r0 : r0 + n, w0:w1]
            b, e = bd[i, : w1 - w0, : t1 - t0], hd[i, : w1 - w0, : t1 - t0]
            qn = qw.astype(F32) * norms[:, w0:w1]
            qa = qn.astype(BF16)
            qb = (qn - qa.astype(F32)).astype(BF16)
            num = jnp.dot(qw, b, preferred_element_type=F32)
            den = jnp.dot(qa, e, preferred_element_type=F32) + jnp.dot(qb, e, preferred_element_type=F32)
            att[r0 : r0 + n, t0:t1] = (num / den).astype(BF16)

    def project(r0, n, edges=False):
        for kh in range(2):
            for a in range(0, KH, 256):
                b = min(a + 256, KH if kh == 0 else 1088)
                cols = slice(kh * KH + a, kh * KH + b)
                p = jnp.dot(att[r0 : r0 + n], ow[:, cols], preferred_element_type=F32)
                p = p + s6[r0 : r0 + n, cols].astype(F32)
                if edges:
                    p = jnp.concatenate([jnp.where(h > 0, p[:160], 0.0), jnp.where(h < 15, p[160:], 0.0)])
                mix[kh, r0 : r0 + n, a:b] = p.astype(BF16)
        mix[1, r0 : r0 + n, 1088:KH] = jnp.zeros((n, KH - 1088), BF16)

    attend(0, 640)
    out_copy = pltpu.make_async_copy(att.at[0:640], att_out, att_sem)
    out_copy.start()
    far_event(0)
    loads[3].wait()
    loads[4].wait()
    project(0, 640)
    far_event(-1)
    x_event(2)
    y_take(zf)
    y_take(at(-1, z)), y_take(at(1, z))
    halos[0].wait_recv()
    halos[1].wait_recv()
    for r in (640, 800):
        q6[r : r + 160] = phi(q6[r : r + 160]).astype(BF16)
    attend(640, 320)
    far_event(1)
    y_take(at(-1, zat(-1))), y_take(at(1, zat(-1)))
    halos[2].wait_recv()
    halos[3].wait_recv()
    project(640, 320, True)

    def block_of(s):
        g = s // 5
        off = jnp.where(g == 2, 3, jnp.where(g == 3, 2, g))
        gx = lax.rem(x + off, 4)
        inner = 11 * (gx // 2) + 6 * lax.rem(gx, 2) + lax.rem(s, 5)
        return jnp.where(s < 20, inner, jnp.where(s == 20, 5, 16))

    def fetch(s):
        b = block_of(s)
        return pltpu.make_async_copy(
            w_all.at[:, :, pl.ds(pl.multiple_of(b * 128, 128), 128)], wbuf.at[lax.rem(s, 2)], wb_sem.at[lax.rem(s, 2)]
        )

    def put(s):
        b = block_of(s)
        return pltpu.make_async_copy(
            obuf.at[lax.rem(s, 2)], gated_out.at[:, :, pl.ds(pl.multiple_of(b * 128, 128), 128)], ob_sem.at[lax.rem(s, 2)]
        )

    zero = jnp.zeros((8, 128), F32)
    for e in (ev, eg):
        for r in range(6):
            e[r, 0:8] = zero
            e[r, 168:176] = zero
    fill.wait()
    d_wait(zm)
    d_wait(zp)
    d_wait(zf)
    fetch(0).start()
    nt = (((1,), (1,)), ((), ()))

    def ready(dx):
        for k in range(4):
            d_wait(at(dx, zat(k)))

    def at_step(s):
        if s == 1:
            y_take(at(-1, zat(1))), y_take(at(1, zat(1)))
        elif s == 2:
            far_event(2)
        elif s == 4:
            y_take(at(-1, zat(2))), y_take(at(1, zat(2))), ready(1)
        elif s == 6:
            y_take(at(2, z)), y_take(at(2, zat(-1)))
        elif s == 9:
            ready(-1)
        elif s == 10:
            y_take(at(2, zat(1)))
        elif s == 12:
            y_take(at(2, zat(2)))
        elif s == 14:
            ready(2)

    events = (1, 2, 4, 6, 9, 10, 12, 14)

    def block(s, _):
        for e in events:
            pl.when(s == e)(functools.partial(at_step, e))
        slot = lax.rem(s, 2)

        @pl.when(s < 21)
        def _():
            fetch(s + 1).start()

        fetch(s).wait()
        b = block_of(s)
        for r0, pair in ((0, (1, 2)), (2, (3, 4)), (4, (0, 5))):
            acc = None
            for kh in range(2):
                w = wbuf[slot, kh].reshape(256, KH)
                t = lax.dot_general(mix[kh, r0 * 160 : (r0 + 2) * 160], w, nt, preferred_element_type=F32)
                acc = t if acc is None else acc + t
            for i, r in enumerate(pair):
                ev[r, 8:168] = acc[i * 160 : (i + 1) * 160, :128]
                eg[r, 8:168] = acc[i * 160 : (i + 1) * 160, 128:]

        @pl.when(s >= 2)
        def _():
            put(s - 2).wait()

        lanes = pl.ds(pl.multiple_of(b * 128, 128), 128)
        taps = [
            [jnp.broadcast_to(cw[pl.ds(i * 2 + j, 1), lanes], (8, 128)) for i in range(9)] for j in range(2)
        ]
        step = 16
        for k in range(0, 160, step):
            sums = []
            for e, w in ((ev, taps[0]), (eg, taps[1])):
                acc = [None] * 4
                for r in range(6):
                    for bb in range(3):
                        v = e[r, k + 7 + bb : k + 7 + bb + step].reshape(step // 8, 8, 128)
                        for a in range(3):
                            o = r - a
                            if 0 <= o < 4:
                                t = (v * w[a * 3 + bb]).reshape(step, 128)
                                acc[o] = t if acc[o] is None else acc[o] + t
                sums.append(acc)
            for o in range(4):
                v, g = sums[0][o], sums[1][o]
                res = (0.5 * v * g) * (1.0 + jnp.tanh(0.5 * g))
                obuf[slot, o, k : k + step] = res.astype(BF16)
        put(s).start()
        return 0

    lax.fori_loop(0, 22, block, 0)
    put(20).wait()
    put(21).wait()
    out_copy.wait()
    edge.wait_send()
    for copy in halos:
        copy.wait_send()
    send(got, got, rs_s, rs_r, tm, h).wait_send()
    send(early, early, pre_s, pre_r, tm, h).wait_send()
    send(full.at[0:15], full.at[0:15], ag_s, ag_r, tm, h).wait_send()
    whole = w_all.at[0, 0, pl.ds(0, 15 * SHARD)]
    for sem in (ring_s, y_s, dr_s, dy_s):
        send(whole, whole, sem, ring_r.at[0], tm, h).wait_send()


def local(stream, query_tokens, key_tokens, value_tokens, out_weight, in_weight, conv_weight):
    height = lax.axis_index("height")
    raw = in_weight.transpose(2, 1, 0)
    blank = jnp.zeros((16, 2, 2240), BF16)

    def packed(rows):
        rows = jnp.pad(rows, ((0, 0), (0, 0), (0, 64))).transpose(1, 0, 2)
        return jnp.stack([rows[:, :, :KH], rows[:, :, KH:]])

    wa = packed(lax.dynamic_slice(jnp.concatenate([raw, blank]), (height, 0, 0), (SHARD, 2, 2240)))
    wb = packed(lax.dynamic_slice(jnp.concatenate([blank, raw[:16]]), (height, 0, 0), (16, 2, 2240)))
    cw = jnp.pad(conv_weight.reshape(18, 2800), ((0, 0), (0, 16)))
    anyspace = pl.BlockSpec(memory_space=pl.ANY)
    vmem = pl.BlockSpec(memory_space=pltpu.VMEM)
    dma, V = pltpu.SemaphoreType.DMA, pltpu.VMEM
    attended, gated, _ = pl.pallas_call(
        kernel,
        in_specs=[anyspace] * 7 + [vmem],
        out_specs=[anyspace] * 3,
        out_shape=[
            jax.ShapeDtypeStruct((TOK, COLS), BF16),
            jax.ShapeDtypeStruct((4, 160, CH), BF16),
            jax.ShapeDtypeStruct((2, 2, CH, KH), BF16),
        ],
        scratch_shapes=[
            V((960, COLS), BF16), V((960, 2240), BF16), V((TOK, COLS), BF16), V((COLS, TOK), BF16), V((TOK, COLS), BF16),
            V((COLS, 2240), BF16), V((2, 2, SHARD, KH), BF16), V((2, 2, 16, KH), BF16), V((960, COLS), BF16), V((2, 960, KH), BF16),
            V((16, 8, KH), BF16), V((15, 8, KH), BF16), V((8, KH), F32), V((7, 8, KH), F32), V((16, 8, KH), BF16),
            V((5, 512, 256), BF16), V((5, 512, 256), BF16),
            V((6, 176, 128), F32), V((6, 176, 128), F32),
            V((2, 2, 2, 128, KH), BF16), V((2, 4, 160, 128), BF16),
            dma((6,)), dma((4,)), dma((4,)),
            dma, dma, dma, dma, dma, dma,
            dma, dma, dma, dma, dma((16,)), dma((16,)), dma((16,)), dma((16,)),
            dma, dma((2,)), dma((2,)), dma, dma, dma,
        ],
        compiler_params=pltpu.CompilerParams(
            collective_id=0, has_side_effects=True, vmem_limit_bytes=60 * 2**20
        ),
    )(
        query_tokens.reshape(TOK, COLS), key_tokens.reshape(TOK, COLS), value_tokens.reshape(TOK, COLS),
        stream.reshape(TOK, 2240), out_weight, wa, wb, cw,
    )
    return attended.reshape(1, 4, 160, COLS), gated[None, :, :, :2800]


def solution(mesh):
    rows = P("tm", "height", None, None)
    return jax.shard_map(
        local,
        mesh=mesh,
        in_specs=(rows, rows, rows, rows, P(), P(None, None, "height"), P()),
        out_specs=(rows, rows),
        check_vma=False,
    )
```

```python
import functools

import jax
import jax.numpy as jnp
from jax import lax
from jax.experimental import pallas as pl
from jax.experimental.pallas import tpu as pltpu
from jax.sharding import PartitionSpec as P

MESH = pl.DeviceIdType.MESH
F32, BF16 = jnp.float32, jnp.bfloat16
HD, TOK, COLS = 112, 640, 1120
SHARD, KH, CH = 176, 1152, 2816
TILES = (
    (0, 256, 0, 384),
    (256, 512, 128, 640),
    (512, 768, 384, 896),
    (768, 1024, 640, 1120),
    (1024, 1120, 896, 1120),
)


def phi(x):
    wide = x.astype(F32)
    return jnp.where(wide > 0, wide + 1.0, jnp.exp(jnp.minimum(wide, 0.0)))


def heads_of(t0, t1):
    return range(t0 // HD, (t1 - 1) // HD + 1)


def lanes_in(head, t0, t1):
    lanes = t0 + lax.broadcasted_iota(jnp.int32, (HD, t1 - t0), 1)
    return (lanes >= head * HD) & (lanes < (head + 1) * HD)


def kernel(
    q_h, k_h, v_h, s_h, ow_h, wa_h, wb_h, cw,
    att_out, gated_out, w_all,
    q6, s6, kk, kt, vv, ow, wp, wx, att, mix, own, got, tot, early, full, bd, hd, ev, eg, wbuf, obuf,
    load_sem, halo_s, halo_r, rs_s, rs_r, pre_s, pre_r, ag_s, ag_r,
    ring_s, y_s, dr_s, dy_s, ring_r, y_r, dr_r, dy_r, fill_sem, wb_sem, ob_sem, att_sem, edge_s, edge_r,
):
    tm, h = lax.axis_index("tm"), lax.axis_index("height")
    y, c = tm // 2, lax.rem(tm, 2)
    x, z = h // 4, lax.rem(h, 4)
    j0 = lax.rem(y, 2)
    j1 = 1 - j0

    loads = [
        pltpu.make_async_copy(k_h, kk, load_sem.at[0]),
        pltpu.make_async_copy(v_h, vv, load_sem.at[1]),
        pltpu.make_async_copy(q_h, q6.at[0:640], load_sem.at[2]),
        pltpu.make_async_copy(s_h, s6.at[0:640], load_sem.at[3]),
        pltpu.make_async_copy(ow_h, ow, load_sem.at[4]),
        pltpu.make_async_copy(wa_h, wp, load_sem.at[5]),
    ]
    fill = pltpu.make_async_copy(wp, w_all.at[:, :, pl.ds(pl.multiple_of(h * SHARD, 16), SHARD)], fill_sem)

    barrier = pltpu.get_barrier_semaphore()

    def greet(d, _):
        pl.semaphore_signal(barrier, inc=1, device_id={"tm": tm, "height": lax.rem(h + d, 16)}, device_id_type=MESH)
        return 0

    def greet_tm(d, _):
        pl.semaphore_signal(barrier, inc=1, device_id={"tm": lax.rem(tm + d, 8), "height": h}, device_id_type=MESH)
        return 0

    lax.fori_loop(1, 16, greet, 0)
    lax.fori_loop(1, 8, greet_tm, 0)
    for i in (5, 0, 1, 2, 3, 4):
        loads[i].start()
    pl.semaphore_wait(barrier, 22)
    up, down = lax.rem(h + 15, 16), lax.rem(h + 1, 16)

    def send(src, dst, ssem, rsem, to_tm, to_h):
        return pltpu.make_async_remote_copy(
            src_ref=src, dst_ref=dst, send_sem=ssem, recv_sem=rsem,
            device_id={"tm": to_tm, "height": to_h}, device_id_type=MESH,
        )

    def at(dx, zz):
        return lax.rem(x + dx + 4, 4) * 4 + zz

    def zat(dz):
        return lax.rem(z + dz + 4, 4)

    def piece(o, kh, j):
        return w_all.at[kh, j, pl.ds(pl.multiple_of(o * SHARD, 16), SHARD)]

    def ring_send(o, to_h, src=None):
        dst = piece(o, c, j0)
        send(dst if src is None else src, dst, ring_s, ring_r.at[o], tm, to_h).start()

    def ring_wait(o):
        send(piece(o, c, j0), piece(o, c, j0), ring_s, ring_r.at[o], tm, h).wait_recv()

    def pass_on(o, over_y=True):
        low = lax.rem(o // 8 + lax.rem(o, 4) // 2, 2)
        yt = lax.rem(y + 3 + 2 * low, 4)
        p = piece(o, c, j0)
        if over_y:
            send(p, p, y_s, y_r.at[o], yt * 2 + c, h).start()
        send(p, p, dr_s, dr_r.at[o], y * 2 + 1 - c, h).start()

    def y_take(o):
        p = piece(o, c, j1)
        send(p, p, y_s, y_r.at[o], tm, h).wait_recv()
        send(p, p, dy_s, dy_r.at[o], y * 2 + 1 - c, h).start()

    def d_wait(o):
        p = piece(o, 1 - c, j0)
        send(p, p, dr_s, dr_r.at[o], tm, h).wait_recv()
        p = piece(o, 1 - c, j1)
        send(p, p, dy_s, dy_r.at[o], tm, h).wait_recv()

    def to_x(o, src=None):
        ring_send(o, at(1, z), src)
        ring_send(o, at(-1, z), src)

    def x_take(k):
        zz = zat(k)
        ring_wait(at(-1, zz))
        ring_wait(at(1, zz))
        pass_on(at(-1, zz))
        pass_on(at(1, zz))

    def x_turn(k):
        zz = zat(k)
        limit = jnp.where(z == 0, 3, jnp.where(z == 3, 1, 2))
        d = jnp.where(zz < limit, 1, -1)
        ring_send(lax.rem(x - d + 4, 4) * 4 + zz, lax.rem(x + d + 4, 4) * 4 + z)

    def x_event(k):
        x_take(k)
        x_turn(k)

    edge = send(wb_h, wx, edge_s, edge_r, tm, up)
    edge.start()
    own[...] = jnp.zeros(own.shape, BF16)
    loads[5].wait()
    edge.wait_recv()
    wp[:, :, 160:176] = wp[:, :, 160:176] + wx[...]
    loads[0].wait()
    for r in range(0, TOK, 160):
        kk[r : r + 160] = phi(kk[r : r + 160]).astype(BF16)
    mine = wp.at[c, j0]
    dz = 1 - 2 * c
    ring_send(h, x * 4 + zat(1), mine)
    ring_send(h, x * 4 + zat(-1), mine)
    to_x(h, mine)
    for d in (1, -1):
        send(wp.at[c, j1], piece(h, c, j1), y_s, y_r.at[h], tm, x * 4 + zat(d)).start()
    fill.start()

    loads[1].wait()
    norm = jnp.sum(kk[...].astype(F32), axis=0, keepdims=True)
    own[14, :, :COLS] = jnp.broadcast_to(norm, (8, COLS)).astype(BF16)
    for a in range(0, COLS, 128):
        b = min(a + 128, COLS)
        kt[a:b] = kk[:, a:b].T
    zm, zp, zf = x * 4 + zat(-1), x * 4 + zat(1), x * 4 + zat(2)
    for i, (t0, t1, w0, w1) in enumerate(TILES):
        if i == 2:
            ring_wait(zm)
            ring_wait(zp)
            ring_send(x * 4 + zat(-dz), x * 4 + zat(dz))
            x_take(0)
            x_turn(0)
            to_x(zm)
            pass_on(zm, False)
        part = jnp.dot(kt[w0:w1], vv[:, t0:t1], preferred_element_type=F32)
        state = jnp.zeros((HD, t1 - t0), F32)
        for head in heads_of(t0, t1):
            a = head * HD - w0
            state = jnp.where(lanes_in(head, t0, t1), part[a : a + HD], state)
        own[0:14, :, t0:t1] = state.reshape(14, 8, t1 - t0).astype(BF16)

    def rs(d, _):
        to = lax.rem(h + d, 16)
        send(own.at[to], got.at[d - 1], rs_s, rs_r, tm, to).start()
        return 0

    lax.fori_loop(1, 16, rs, 0)

    to_x(zp)
    pass_on(zp, False)
    y_take(zm)
    y_take(zp)
    turn = piece(x * 4 + zat(-dz), c, j1)
    send(turn, turn, y_s, y_r.at[x * 4 + zat(-dz)], tm, x * 4 + zat(dz)).start()
    loads[2].wait()
    for r in range(0, TOK, 160):
        q6[r : r + 160] = phi(q6[r : r + 160]).astype(BF16)

    send(got, got, rs_s, rs_r, tm, h).wait_recv()
    tot[...] = own[h].astype(F32) + jnp.sum(got[...].astype(F32), axis=0)

    def pre(d, _):
        send(tot, early.at[d - 1], pre_s, pre_r, lax.rem(tm + d, 8), h).start()
        return 0

    lax.fori_loop(1, 8, pre, 0)
    halos = [
        send(q_h.at[480:640], q6.at[640:800], halo_s.at[0], halo_r.at[0], tm, down),
        send(q_h.at[0:160], q6.at[800:960], halo_s.at[1], halo_r.at[1], tm, up),
        send(s_h.at[480:640], s6.at[640:800], halo_s.at[2], halo_r.at[2], tm, down),
        send(s_h.at[0:160], s6.at[800:960], halo_s.at[3], halo_r.at[3], tm, up),
    ]
    halos[0].start()
    halos[1].start()
    x_take(-1)
    send(early, early, pre_s, pre_r, tm, h).wait_recv()
    causal = tot[...]
    for d in range(1, 8):
        causal = causal + jnp.where(d <= tm, early[d - 1], 0.0)
    high = causal.astype(BF16)
    rest = (causal - high.astype(F32)).astype(BF16)
    odd = lax.broadcasted_iota(jnp.int32, causal.shape, 0) == 1
    full[h] = jnp.where(odd & (h == 14), rest.astype(F32), high.astype(F32)).astype(BF16)

    def ag(d, _):
        to = lax.rem(h + d, 16)
        send(full.at[h], full.at[h], ag_s, ag_r, tm, to).start()
        return 0

    lax.fori_loop(1, 16, ag, 0)
    halos[2].start()
    halos[3].start()

    def far_event(k):
        ring_wait(at(2, zat(k)))
        pass_on(at(2, zat(k)))

    x_turn(-1)
    ring_wait(zf)
    to_x(zf)
    pass_on(zf, False)
    x_event(1)

    send(full.at[0:15], full.at[0:15], ag_s, ag_r, tm, h).wait_recv()
    for i, (t0, t1, w0, w1) in enumerate(TILES):
        bd[i] = jnp.zeros(bd.shape[1:], BF16)
        hd[i] = jnp.zeros(hd.shape[1:], BF16)
        state = full[0:14, :, t0:t1].astype(F32).reshape(HD, t1 - t0)
        for head in heads_of(t0, t1):
            a, inside = head * HD - w0, lanes_in(head, t0, t1)
            bd[i, a : a + HD, : t1 - t0] = jnp.where(inside, state, 0.0).astype(BF16)
            hd[i, a : a + HD, : t1 - t0] = jnp.where(inside, 1.0, 0.0).astype(BF16)
    norms = full[14, 0:1, :COLS].astype(F32) + full[14, 1:2, :COLS].astype(F32)

    def attend(r0, n):
        for i, (t0, t1, w0, w1) in enumerate(TILES):
            qw = q6[r0 : r0 + n, w0:w1]
            b, e = bd[i, : w1 - w0, : t1 - t0], hd[i, : w1 - w0, : t1 - t0]
            qn = qw.astype(F32) * norms[:, w0:w1]
            qa = qn.astype(BF16)
            qb = (qn - qa.astype(F32)).astype(BF16)
            num = jnp.dot(qw, b, preferred_element_type=F32)
            den = jnp.dot(qa, e, preferred_element_type=F32) + jnp.dot(qb, e, preferred_element_type=F32)
            att[r0 : r0 + n, t0:t1] = (num / den).astype(BF16)

    def project(r0, n, edges=False):
        for kh in range(2):
            for a in range(0, KH, 256):
                b = min(a + 256, KH if kh == 0 else 1088)
                cols = slice(kh * KH + a, kh * KH + b)
                p = jnp.dot(att[r0 : r0 + n], ow[:, cols], preferred_element_type=F32)
                p = p + s6[r0 : r0 + n, cols].astype(F32)
                if edges:
                    p = jnp.concatenate([jnp.where(h > 0, p[:160], 0.0), jnp.where(h < 15, p[160:], 0.0)])
                mix[kh, r0 : r0 + n, a:b] = p.astype(BF16)
        mix[1, r0 : r0 + n, 1088:KH] = jnp.zeros((n, KH - 1088), BF16)

    attend(0, 640)
    out_copy = pltpu.make_async_copy(att.at[0:640], att_out, att_sem)
    out_copy.start()
    far_event(0)
    loads[3].wait()
    loads[4].wait()
    project(0, 640)
    far_event(-1)
    x_event(2)
    y_take(zf)
    y_take(at(-1, z)), y_take(at(1, z))
    halos[0].wait_recv()
    halos[1].wait_recv()
    for r in (640, 800):
        q6[r : r + 160] = phi(q6[r : r + 160]).astype(BF16)
    attend(640, 320)
    far_event(1)
    y_take(at(-1, zat(-1))), y_take(at(1, zat(-1)))
    halos[2].wait_recv()
    halos[3].wait_recv()
    project(640, 320, True)

    def block_of(s):
        g = s // 5
        off = jnp.where(g == 2, 3, jnp.where(g == 3, 2, g))
        gx = lax.rem(x + off, 4)
        inner = 11 * (gx // 2) + 6 * lax.rem(gx, 2) + lax.rem(s, 5)
        return jnp.where(s < 20, inner, jnp.where(s == 20, 5, 16))

    def fetch(s):
        b = block_of(s)
        return pltpu.make_async_copy(
            w_all.at[:, :, pl.ds(pl.multiple_of(b * 128, 128), 128)], wbuf.at[lax.rem(s, 2)], wb_sem.at[lax.rem(s, 2)]
        )

    def put(s):
        b = block_of(s)
        return pltpu.make_async_copy(
            obuf.at[lax.rem(s, 2)], gated_out.at[:, :, pl.ds(pl.multiple_of(b * 128, 128), 128)], ob_sem.at[lax.rem(s, 2)]
        )

    zero = jnp.zeros((8, 128), F32)
    for e in (ev, eg):
        for r in range(6):
            e[r, 0:8] = zero
            e[r, 168:176] = zero
    fill.wait()
    d_wait(zm)
    d_wait(zp)
    d_wait(zf)
    fetch(0).start()
    nt = (((1,), (1,)), ((), ()))

    def ready(dx):
        for k in range(4):
            d_wait(at(dx, zat(k)))

    def at_step(s):
        if s == 1:
            y_take(at(-1, zat(1))), y_take(at(1, zat(1)))
        elif s == 2:
            far_event(2)
        elif s == 4:
            y_take(at(-1, zat(2))), y_take(at(1, zat(2))), ready(1)
        elif s == 6:
            y_take(at(2, z)), y_take(at(2, zat(-1)))
        elif s == 9:
            ready(-1)
        elif s == 10:
            y_take(at(2, zat(1)))
        elif s == 12:
            y_take(at(2, zat(2)))
        elif s == 14:
            ready(2)

    events = (1, 2, 4, 6, 9, 10, 12, 14)

    def block(s, _):
        for e in events:
            pl.when(s == e)(functools.partial(at_step, e))
        slot = lax.rem(s, 2)

        @pl.when(s < 21)
        def _():
            fetch(s + 1).start()

        fetch(s).wait()
        b = block_of(s)
        for r0, pair in ((0, (1, 2)), (2, (3, 4)), (4, (0, 5))):
            acc = None
            for kh in range(2):
                w = wbuf[slot, kh].reshape(256, KH)
                t = lax.dot_general(mix[kh, r0 * 160 : (r0 + 2) * 160], w, nt, preferred_element_type=F32)
                acc = t if acc is None else acc + t
            for i, r in enumerate(pair):
                ev[r, 8:168] = acc[i * 160 : (i + 1) * 160, :128]
                eg[r, 8:168] = acc[i * 160 : (i + 1) * 160, 128:]

        @pl.when(s >= 2)
        def _():
            put(s - 2).wait()

        lanes = pl.ds(pl.multiple_of(b * 128, 128), 128)
        taps = [
            [jnp.broadcast_to(cw[pl.ds(i * 2 + j, 1), lanes], (8, 128)) for i in range(9)] for j in range(2)
        ]
        step = 16
        for k in range(0, 160, step):
            sums = []
            for e, w in ((ev, taps[0]), (eg, taps[1])):
                acc = [None] * 4
                for r in range(6):
                    for bb in range(3):
                        v = e[r, k + 7 + bb : k + 7 + bb + step].reshape(step // 8, 8, 128)
                        for a in range(3):
                            o = r - a
                            if 0 <= o < 4:
                                t = (v * w[a * 3 + bb]).reshape(step, 128)
                                acc[o] = t if acc[o] is None else acc[o] + t
                sums.append(acc)
            for o in range(4):
                v, g = sums[0][o], sums[1][o]
                res = (0.5 * v * g) * (1.0 + jnp.tanh(0.5 * g))
                obuf[slot, o, k : k + step] = res.astype(BF16)
        put(s).start()
        return 0

    lax.fori_loop(0, 22, block, 0)
    put(20).wait()
    put(21).wait()
    out_copy.wait()
    edge.wait_send()
    for copy in halos:
        copy.wait_send()
    send(got, got, rs_s, rs_r, tm, h).wait_send()
    send(early, early, pre_s, pre_r, tm, h).wait_send()
    send(full.at[0:15], full.at[0:15], ag_s, ag_r, tm, h).wait_send()
    whole = w_all.at[0, 0, pl.ds(0, 15 * SHARD)]
    for sem in (ring_s, y_s, dr_s, dy_s):
        send(whole, whole, sem, ring_r.at[0], tm, h).wait_send()


def local(stream, query_tokens, key_tokens, value_tokens, out_weight, in_weight, conv_weight):
    height = lax.axis_index("height")
    raw = in_weight.transpose(2, 1, 0)
    blank = jnp.zeros((16, 2, 2240), BF16)

    def packed(rows):
        rows = jnp.pad(rows, ((0, 0), (0, 0), (0, 64))).transpose(1, 0, 2)
        return jnp.stack([rows[:, :, :KH], rows[:, :, KH:]])

    wa = packed(lax.dynamic_slice(jnp.concatenate([raw, blank]), (height, 0, 0), (SHARD, 2, 2240)))
    wb = packed(lax.dynamic_slice(jnp.concatenate([blank, raw[:16]]), (height, 0, 0), (16, 2, 2240)))
    cw = jnp.pad(conv_weight.reshape(18, 2800), ((0, 0), (0, 16)))
    anyspace = pl.BlockSpec(memory_space=pl.ANY)
    vmem = pl.BlockSpec(memory_space=pltpu.VMEM)
    dma, V = pltpu.SemaphoreType.DMA, pltpu.VMEM
    attended, gated, _ = pl.pallas_call(
        kernel,
        in_specs=[anyspace] * 7 + [vmem],
        out_specs=[anyspace] * 3,
        out_shape=[
            jax.ShapeDtypeStruct((TOK, COLS), BF16),
            jax.ShapeDtypeStruct((4, 160, CH), BF16),
            jax.ShapeDtypeStruct((2, 2, CH, KH), BF16),
        ],
        scratch_shapes=[
            V((960, COLS), BF16), V((960, 2240), BF16), V((TOK, COLS), BF16), V((COLS, TOK), BF16), V((TOK, COLS), BF16),
            V((COLS, 2240), BF16), V((2, 2, SHARD, KH), BF16), V((2, 2, 16, KH), BF16), V((960, COLS), BF16), V((2, 960, KH), BF16),
            V((16, 8, KH), BF16), V((15, 8, KH), BF16), V((8, KH), F32), V((7, 8, KH), F32), V((16, 8, KH), BF16),
            V((5, 512, 256), BF16), V((5, 512, 256), BF16),
            V((6, 176, 128), F32), V((6, 176, 128), F32),
            V((2, 2, 2, 128, KH), BF16), V((2, 4, 160, 128), BF16),
            dma((6,)), dma((4,)), dma((4,)),
            dma, dma, dma, dma, dma, dma,
            dma, dma, dma, dma, dma((16,)), dma((16,)), dma((16,)), dma((16,)),
            dma, dma((2,)), dma((2,)), dma, dma, dma,
        ],
        compiler_params=pltpu.CompilerParams(
            collective_id=0, has_side_effects=True, vmem_limit_bytes=60 * 2**20
        ),
    )(
        query_tokens.reshape(TOK, COLS), key_tokens.reshape(TOK, COLS), value_tokens.reshape(TOK, COLS),
        stream.reshape(TOK, 2240), out_weight, wa, wb, cw,
    )
    return attended.reshape(1, 4, 160, COLS), gated[None, :, :, :2800]


def solution(mesh):
    rows = P("tm", "height", None, None)
    return jax.shard_map(
        local,
        mesh=mesh,
        in_specs=(rows, rows, rows, rows, P(), P(None, None, "height"), P()),
        out_specs=(rows, rows),
        check_vma=False,
    )
```
